256 devices in a mesh: grp: 4 (over y), seq: 32 (over z, x), tp: 2 (over core).
Axes of the slice: x: 4, y: 4, z: 8, core: 2. Of those that a mesh axis runs over, the one named last changes fastest.
Arguments:
- hidden_in: bfloat16 [4, 16384, 1792], P('grp', 'seq'), may hold values from -8 to 8
- norm_gain: float32 [1792], replicated, may hold values from 0.5 to 1.5
- w_feature: bfloat16 [1792, 256], P(None, 'tp'), may hold values from -0.125 to 0.125
- w_value: bfloat16 [1792, 1792], P(None, 'tp'), may hold values from -0.125 to 0.125
- w_window: bfloat16 [1792, 1792], P(None, 'tp'), may hold values from -0.125 to 0.125
- w_out: bfloat16 [1792, 1792], P('tp'), may hold values from -0.125 to 0.125
- prefix_state: float32 [4, 32, 8, 153, 112], P('grp', 'seq', 'tp'), may hold values from -36864 to 36864
- prefix_norm: float32 [4, 32, 8, 153], P('grp', 'seq', 'tp'), may hold values from -409.6 to 8192, as said below
- prefix_kv: bfloat16 [4, 32, 64, 1792], P('grp', 'seq', None, 'tp'), may hold values from -6 to 6
- lengths: int32 [4, 8], P('grp'), may hold values from 1 to 8192, 16384 in all within a row
- prefix_owner: int32 [4], replicated, may hold values from 0 to 31
- row_group: int32 [4], replicated, may hold values from 0 to 3, each once
Outputs:
- hidden_out: float32 [4, 16384, 1792], P('grp', 'seq', 'tp')
The draws below stay inside these ranges and needn't reach their ends.
Inputs may be any that keep to these rules, and one draw needn't show every extreme that they name: `lengths`: each row sums to 16384 and its largest length is exactly 8192. `prefix_owner`: a slot index along seq. `row_group`: a permutation of the groups. `prefix_norm`: the first entry of each row is 8192, the count of prefix tokens; phi(q) . prefix_norm is positive for every query q.
All inputs are finite; a program needn't handle non-finite values.
Results may differ from the reference program's by a relative error of at most 0.0017.
Values may be sent and summed in bfloat16 or wider, within the bound.
A program may use at most 256 MiB of HBM per device.

```python
import math
import jax
import jax.numpy as jnp
import numpy as np
from jax import lax

D = 1792
HEADS = 8
HD = 112
FD = 16
NF = 153
WIN = 64
PREFIX = 8192
REQ = 8
TOK_DEV = 512
GROUPS = 4
SLOTS = 32
TOK = 16384
MOST = 8192


def feature_means(key):
    rng_keys = jax.random.split(jax.random.fold_in(key, 11), 3)
    lead = (GROUPS, SLOTS, HEADS)
    first_idx, second_idx = np.triu_indices(FD)
    on_diagonal = jnp.asarray(first_idx == second_idx)
    pair_count = first_idx.shape[0]
    constant = jnp.ones(lead + (1,), jnp.float32)
    linear = jax.random.uniform(rng_keys[0], lead + (FD,), jnp.float32, -0.05, 0.05)
    quad_diag = jax.random.uniform(rng_keys[1], lead + (pair_count,), jnp.float32, 0.15, 0.3)
    quad_off = jax.random.uniform(rng_keys[2], lead + (pair_count,), jnp.float32, -0.002, 0.002)
    quadratic = jnp.where(on_diagonal, quad_diag, quad_off)
    return jnp.concatenate([constant, linear, quadratic], axis=-1)


def draw_prefix_norm(key, part):
    return (feature_means(key) * PREFIX).astype(jnp.float32)


def draw_prefix_state(key, part):
    means = feature_means(key)
    rng_keys = jax.random.split(jax.random.fold_in(key, 23), 2)
    lead = (GROUPS, SLOTS, HEADS)
    pair_count = FD * (FD + 1) // 2
    feature_spread = jnp.asarray(np.concatenate([np.full((1,), 0.5), np.full((FD,), 0.3), np.full((pair_count,), 0.1)]).astype(np.float32))
    value_mean = jnp.clip(jax.random.normal(rng_keys[0], lead + (1, HD), jnp.float32), -3.0, 3.0)
    spread = jnp.clip(jax.random.normal(rng_keys[1], lead + (NF, HD), jnp.float32), -3.0, 3.0)
    state = means[..., None] * value_mean + feature_spread[:, None] * spread
    return (state * PREFIX).astype(jnp.float32)


def draw_hidden_in(key, part):
    rng_keys = jax.random.split(jax.random.fold_in(key, 37), 2)
    common = 0.8 * jnp.clip(jax.random.normal(rng_keys[0], (GROUPS, 1, D), jnp.float32), -3.0, 3.0)
    noise = jnp.clip(jax.random.normal(rng_keys[1], (GROUPS, TOK, D), jnp.float32), -6.0, 6.0)
    return jnp.clip(common + noise, -8.0, 8.0).astype(jnp.bfloat16)


def with_ends(array, own_key, smallest, top_value):
    longest = array.shape.index(max(array.shape))
    spots = []
    for shift in (0, 1):
        where = [jax.random.randint(jax.random.fold_in(own_key, axis), (), 0, length) for axis, length in enumerate(array.shape)]
        where[longest] = (where[longest] + shift) % array.shape[longest]
        spots.append(tuple(where))
    return array.at[spots[0]].set(smallest).at[spots[1]].set(top_value)


def steps_of(rng, extent, cuts, least, top_value):
    def one(axis_at, blocks):
        heights = jax.random.uniform(jax.random.fold_in(jax.random.fold_in(rng, 6), axis_at), (blocks,), jnp.float32, least / len(cuts), top_value / len(cuts))
        return jnp.repeat(jnp.exp(heights), extent[axis_at] // blocks).reshape((-1,) + (1,) * (len(extent) - axis_at - 1))

    loudness = one(*cuts[0])
    for cut in cuts[1:]:
        loudness = loudness * one(*cut)
    return loudness


def length_profile(amount, total, limit, lean):
    loads = [(1 << 20) // math.isqrt(grade ** lean) + 1 for grade in range(2, amount + 1)]
    spare, holding = total - limit - (amount - 1), [1] * (amount - 1)
    while spare > 0:
        candidates = [i for i in range(amount - 1) if holding[i] < limit]
        pool, budget = sum([loads[i] for i in candidates]), spare
        for i in candidates:
            addition = min(limit - holding[i], max(1, budget * loads[i] // pool), spare)
            holding[i] = holding[i] + addition
            spare = spare - addition
    return np.array([limit] + holding)


def ragged(own_key, count, total, bound, lean):
    if count == 2:
        one = jax.random.randint(own_key, (), max(1, total - bound), min(bound, total - 1) + 1)
        return jnp.stack([one, total - one])
    sizes = jnp.asarray(length_profile(count, total, bound, lean), jnp.int32)
    couples = (count - 1) // 2
    donor, sink = sizes[1:1 + 2 * couples:2], sizes[2:2 + 2 * couples:2]
    slack = jnp.minimum(donor - 1, bound - sink)
    passed = jax.random.randint(jax.random.fold_in(own_key, 1), (couples,), 0, 1 << 20) % (slack + 1)
    sizes = sizes.at[1:1 + 2 * couples:2].set(donor - passed).at[2:2 + 2 * couples:2].set(sink + passed)
    return sizes[jax.random.permutation(jax.random.fold_in(own_key, 2), count)]


def normal_values(key, shape, scale, reach, cuts=(), kind=jnp.bfloat16):
    drawn = jax.random.normal(key, shape, jnp.float32) * scale
    if len(cuts) > 0:
        drawn = steps_of(key, shape, cuts, -0.22, 0.18) * drawn
    return jnp.clip(drawn, min=-reach, max=reach).astype(kind)


def setup_inputs(seed: int = 0) -> dict:
    key_list = jax.random.split(jax.random.key(seed), 13)
    return {
        "hidden_in": draw_hidden_in(jax.random.fold_in(key_list[12], 71), 0),
        "norm_gain": jnp.clip(1.0 + 0.1 * jax.random.normal(key_list[1], (D,), jnp.float32), 0.5, 1.5),
        "w_feature": normal_values(key_list[2], (D, HEADS * 2 * FD), D ** -0.5, 0.125, ((1, 2),)),
        "w_value": normal_values(key_list[3], (D, HEADS * 2 * HD), D ** -0.5, 0.125, ((1, 2),)),
        "w_window": normal_values(key_list[4], (D, HEADS * 2 * HD), D ** -0.5, 0.125, ((1, 2),)),
        "w_out": normal_values(key_list[5], (HEADS * 2 * HD, D), (HEADS * 2 * HD) ** -0.5, 0.125, ((0, 2),)),
        "prefix_state": draw_prefix_state(jax.random.fold_in(key_list[12], 71), 0),
        "prefix_norm": draw_prefix_norm(jax.random.fold_in(key_list[12], 71), 0),
        "prefix_kv": normal_values(key_list[8], (GROUPS, SLOTS, WIN, HEADS * 2 * HD), 1.0, 6.0, ((0, 4), (1, 32), (3, 2))),
        "lengths": jax.vmap(lambda own: ragged(own, REQ, TOK, MOST, 2))(jax.random.split(key_list[9], GROUPS)).reshape((GROUPS, REQ)).astype(jnp.int32),
        "prefix_owner": with_ends(jax.random.randint(key_list[10], (GROUPS,), 0, SLOTS), jax.random.fold_in(key_list[10], 1), 0, SLOTS - 1).astype(jnp.int32),
        "row_group": jax.random.permutation(key_list[11], GROUPS).astype(jnp.int32),
    }


epsilon = 1e-05
highest = lax.Precision.HIGHEST

def taylor(x):
    width = x.shape[-1]
    first_idx, second_idx = np.triu_indices(width)
    pair_weight = np.where(first_idx == second_idx, 1.0 / math.sqrt(2.0 * width), 1.0 / math.sqrt(width)).astype(np.float32)
    unit_col = jnp.ones(x.shape[:-1] + (1,), jnp.float32)
    return jnp.concatenate([unit_col, x * (1.0 / width ** 0.25), x[..., first_idx] * x[..., second_idx] * pair_weight], axis=-1)

def request_start(places, starts):
    return lax.optimization_barrier(jnp.max(jnp.where(starts[None, :] <= places[:, None], starts[None, :], 0), axis=1))

def project(hidden_rows, norm_gain, w_feature, w_value, w_window, head_count):
    x = hidden_rows.astype(jnp.float32)
    inv_rms = lax.rsqrt(lax.optimization_barrier(jnp.mean(x * x, axis=1, keepdims=True)) + epsilon)
    normed = (x * inv_rms * norm_gain).astype(jnp.bfloat16)
    count = x.shape[0]
    features = jnp.dot(normed, w_feature, preferred_element_type=jnp.float32).reshape(count, head_count, 2, -1)
    values = jnp.dot(normed, w_value, preferred_element_type=jnp.float32).astype(jnp.bfloat16).reshape(count, head_count, 2, -1)
    window = jnp.dot(normed, w_window, preferred_element_type=jnp.float32).astype(jnp.bfloat16).reshape(count, head_count, 2, -1)
    return (features[:, :, 0], features[:, :, 1], values[:, :, 0], values[:, :, 1], window[:, :, 0], window[:, :, 1])

def linear_block(query_feat, key_feat, lin_vals, starts_tok, places, base_state, base_norm, carried_state, carried_norm, use_carry):
    phi_query = taylor(query_feat)
    value_full = lin_vals.astype(jnp.float32)
    numerator = jnp.einsum('thf,hfd->thd', phi_query, base_state, precision=highest) + use_carry[:, None, None] * jnp.einsum('thf,hfd->thd', phi_query, carried_state, precision=highest)
    denominator = jnp.einsum('thf,hf->th', phi_query, base_norm, precision=highest) + use_carry[:, None] * jnp.einsum('thf,hf->th', phi_query, carried_norm, precision=highest)
    similar = jnp.einsum('thf,shf->hts', query_feat, key_feat, precision=highest) * (1.0 / math.sqrt(query_feat.shape[-1]))
    allowed = (starts_tok[:, None] == starts_tok[None, :]) & (places[None, :] <= places[:, None])
    kernel = jnp.where(allowed[None], 1.0 + similar + 0.5 * similar * similar, 0.0)
    numerator = numerator + jnp.einsum('hts,shd->thd', kernel, value_full, precision=highest)
    denominator = denominator + jnp.transpose(lax.optimization_barrier(jnp.sum(kernel, axis=2)))
    return (numerator / denominator[:, :, None]).astype(jnp.bfloat16)

def block_state(key_feat, lin_vals, in_range):
    phi_key = taylor(key_feat) * in_range[:, None, None]
    state_sum = jnp.einsum('thf,thd->hfd', phi_key, lin_vals.astype(jnp.float32), precision=highest)
    return (state_sum, lax.optimization_barrier(jnp.sum(phi_key, axis=0)))

def window_block(win_query, win_keys, win_vals, rim_keys, rim_vals, prefix_keys, prefix_vals, starts_tok, places, anchor):
    span = prefix_keys.shape[0]
    key_rows = jnp.concatenate([prefix_keys, rim_keys, win_keys], axis=0).astype(jnp.float32)
    value_rows = jnp.concatenate([prefix_vals, rim_vals, win_vals], axis=0).astype(jnp.float32)
    later = jnp.arange(span + places.shape[0], dtype=jnp.int32) + (anchor - span)
    band = (later[None, :] <= places[:, None]) & (later[None, :] > places[:, None] - span) & (later[None, :] >= starts_tok[:, None])
    early = jnp.arange(span, dtype=jnp.int32)[None, :] >= (places - starts_tok)[:, None] + 1
    allowed = jnp.concatenate([early, band], axis=1)
    scores = jnp.einsum('thd,khd->htk', win_query.astype(jnp.float32), key_rows) * (1.0 / math.sqrt(win_query.shape[-1]))
    scores = jnp.where(allowed[None], scores, -1e+30)
    top_score = lax.optimization_barrier(jnp.max(scores, axis=2, keepdims=True))
    weights = jnp.exp(scores - top_score)
    weights = (weights / lax.optimization_barrier(jnp.sum(weights, axis=2, keepdims=True))).astype(jnp.bfloat16)
    return jnp.einsum('htk,khd->thd', weights.astype(jnp.float32), value_rows).astype(jnp.bfloat16)

def reference(hidden_in, norm_gain, w_feature, w_value, w_window, w_out, prefix_state, prefix_norm, prefix_kv, lengths, prefix_owner, row_group):
    outcomes = []
    block_count = TOK // TOK_DEV
    for row_index in range(GROUPS):
        group_index = row_group[row_index]
        owner_slot = prefix_owner[group_index]
        base_state = prefix_state[group_index, owner_slot]
        base_norm = prefix_norm[group_index, owner_slot]
        cache_rows = prefix_kv[group_index, owner_slot].reshape(WIN, HEADS, 2, HD)
        query_feat, key_feat, lin_vals, win_vals, win_query, win_keys = project(hidden_in[row_index], norm_gain, w_feature, w_value, w_window, HEADS)
        lengths_row = lengths[row_index]
        starts = (jnp.cumsum(lengths_row) - lengths_row).astype(jnp.int32)
        places = jnp.arange(TOK, dtype=jnp.int32)
        starts_tok = request_start(places, starts).astype(jnp.int32)

        def blocked(a):
            return a.reshape((block_count, TOK_DEV) + a.shape[1:])

        def linear_step(carried, inputs):
            carried_state, carried_norm = carried
            query_part, key_part, value_part, start_part, place_part = inputs
            anchor = place_part[0]
            use_carry = (start_part < anchor).astype(jnp.float32)
            outcome = linear_block(query_part, key_part, value_part, start_part, place_part, base_state, base_norm, carried_state, carried_norm, use_carry)
            in_last = (start_part == start_part[-1]).astype(jnp.float32)
            part_state, part_norm = block_state(key_part, value_part, in_last)
            restart = (start_part[-1] >= anchor).astype(jnp.float32)
            return (((1.0 - restart) * carried_state + part_state, (1.0 - restart) * carried_norm + part_norm), outcome)
        zero_state = jnp.zeros((HEADS, NF, HD), jnp.float32)
        zero_norm = jnp.zeros((HEADS, NF), jnp.float32)
        _, lin_out = lax.scan(linear_step, (zero_state, zero_norm), (blocked(query_feat), blocked(key_feat), blocked(lin_vals), blocked(starts_tok), blocked(places)))
        lin_out = lin_out.reshape(TOK, HEADS, HD)
        padded_keys = jnp.concatenate([jnp.zeros((WIN, HEADS, HD), win_keys.dtype), win_keys], axis=0)
        padded_vals = jnp.concatenate([jnp.zeros((WIN, HEADS, HD), win_vals.dtype), win_vals], axis=0)

        def window_step(block_index):
            anchor = (block_index * TOK_DEV).astype(jnp.int32)
            return window_block(lax.dynamic_slice_in_dim(win_query, anchor, TOK_DEV, 0), lax.dynamic_slice_in_dim(win_keys, anchor, TOK_DEV, 0), lax.dynamic_slice_in_dim(win_vals, anchor, TOK_DEV, 0), lax.dynamic_slice_in_dim(padded_keys, anchor, WIN, 0), lax.dynamic_slice_in_dim(padded_vals, anchor, WIN, 0), cache_rows[:, :, 0], cache_rows[:, :, 1], lax.dynamic_slice_in_dim(starts_tok, anchor, TOK_DEV, 0), lax.dynamic_slice_in_dim(places, anchor, TOK_DEV, 0), anchor)
        win_out = lax.map(window_step, jnp.arange(block_count, dtype=jnp.int32)).reshape(TOK, HEADS, HD)
        attended = jnp.stack([lin_out, win_out], axis=2).reshape(TOK, HEADS * 2 * HD)
        mixed_out = jnp.dot(attended, w_out, preferred_element_type=jnp.float32)
        outcomes.append(hidden_in[row_index].astype(jnp.float32) + mixed_out)
    return jnp.stack(outcomes)
```

```python
import functools
import math

import jax
import jax.numpy as jnp
import numpy as np
from jax import lax
from jax.experimental import pallas as pl
from jax.experimental.pallas import tpu as pltpu
from jax.sharding import PartitionSpec as P

MESH = pl.DeviceIdType.MESH
LANES = 128
CHUNK = 32
KV_CHUNK = 16
f32, bf16 = jnp.float32, jnp.bfloat16


def feature_tables(heads, fd, padded):
    first, second = np.triu_indices(fd)
    count = 1 + fd + len(first)
    rows = np.zeros((8, heads * padded), np.float32)
    rows[0:4] = -1.0
    for h in range(heads):
        at = h * padded
        rows[4, at] = rows[5, at] = rows[6, at] = 1.0
        for kind in range(2):
            base = h * 2 * fd + kind * fd
            rows[2 * kind, at + 1 : at + 1 + fd] = base + np.arange(fd)
            rows[2 * kind, at + 1 + fd : at + count] = base + first
            rows[2 * kind + 1, at + 1 + fd : at + count] = base + second
        rows[5, at + 1 : at + 1 + fd] = 1.0
        rows[6, at + 1 : at + 1 + fd] = 1.0 / fd**0.25
        rows[6, at + 1 + fd : at + count] = np.where(
            first == second, 1.0 / math.sqrt(2.0 * fd), 1.0 / math.sqrt(fd)
        )
    return rows


def split_norm(x, ones_lane):
    lane = lax.broadcasted_iota(jnp.int32, x.shape, x.ndim - 1)
    lost = x - x.astype(bf16).astype(f32)
    moved = pltpu.roll(lost, 1, x.ndim - 1)
    return jnp.where(lane == ones_lane + 1, x + moved, x).astype(bf16)


def start_offsets(starts_ref, anchor, rows, first):
    place = lax.broadcasted_iota(jnp.int32, (rows, 1), 0) + (first + anchor)
    best = jnp.zeros((rows, 1), jnp.int32)
    for r in range(starts_ref.shape[0]):
        best = jnp.maximum(best, jnp.where(starts_ref[r] <= place, starts_ref[r], 0))
    return best - anchor


def project_body(
    starts_ref, hidden, gain, w_feature, w_value, w_window, state, norm, kv, tab_row, tab_col,
    phi_q, feat, feat_t, lin_vals, win_q, win_kv, cache, parts,
    normed, wide,
):
    rows, width = hidden.shape
    heads, nf, hd = state.shape
    padded = parts.shape[0] * CHUNK // heads
    anchor = lax.axis_index("seq") * rows
    per_head = padded // CHUNK
    for h in range(heads):
        body = jnp.concatenate(
            [state[h], norm[h], jnp.zeros((nf, LANES - hd - 1), f32)], axis=1
        )
        body = jnp.concatenate([body, jnp.zeros((padded - nf, LANES), f32)], axis=0)
        cache[h * per_head : (h + 1) * per_head, 0:CHUNK, :] = split_norm(body, hd).reshape(
            per_head, CHUNK, LANES
        )
    span = kv.shape[0]
    blocks = span // KV_CHUNK
    for i in range(2 * heads):
        piece = jnp.concatenate(
            [kv[:, i * hd : (i + 1) * hd], jnp.zeros((span, LANES - hd), bf16)], axis=1
        )
        cache[i * blocks : (i + 1) * blocks, CHUNK:, :] = piece.reshape(blocks, KV_CHUNK, LANES)
    step = 64

    def norm_rows(i, carry):
        at = pl.ds(pl.multiple_of(i * step, step), step)
        x = hidden[at, :].astype(f32)
        inv = lax.rsqrt(jnp.mean(x * x, axis=1, keepdims=True) + 1e-5)
        normed[at, :] = (x * inv * gain[...]).astype(bf16)
        return carry

    lax.fori_loop(0, rows // step, norm_rows, 0)
    feats = jnp.dot(normed[...], w_feature[...], preferred_element_type=f32)
    feats_t = jnp.transpose(feats)
    hi = feats.astype(bf16)
    both = jnp.concatenate([hi, (feats - hi.astype(f32)).astype(bf16)], axis=1)
    hi_t = feats_t.astype(bf16)
    both_t = jnp.concatenate([hi_t, (feats_t - hi_t.astype(f32)).astype(bf16)], axis=0)
    feat[...] = hi
    feat_t[...] = hi_t
    channels = hi.shape[1]
    total = heads * padded
    for n in range(heads):
        at = slice(n * padded, (n + 1) * padded)
        channel = (
            lax.broadcasted_iota(jnp.int32, (2 * channels, padded), 0) % channels
        ).astype(f32)
        one = jnp.where(channel == tab_row[0:1, at], 1.0, 0.0).astype(bf16)
        two = jnp.where(channel == tab_row[1:2, at], 1.0, 0.0).astype(bf16)
        left = jnp.dot(both, one, preferred_element_type=f32) + tab_row[4:5, at]
        right = jnp.dot(both, two, preferred_element_type=f32) + tab_row[5:6, at]
        phi_q[:, at] = (left * right * tab_row[6:7, at]).astype(bf16)
    for lo in range(0, w_value.shape[1], 256):
        up = min(lo + 256, w_value.shape[1])
        wide[:, lo:up] = jnp.dot(
            normed[...], w_value[:, lo:up], preferred_element_type=f32
        ).astype(bf16)
    lane = lax.broadcasted_iota(jnp.int32, (rows, LANES - hd), 1)
    ones = jnp.where(lane == 0, 1.0, 0.0).astype(bf16)
    zeros = jnp.zeros((rows, LANES - hd), bf16)
    for h in range(heads):
        at = 2 * h * hd
        lin_vals[h] = jnp.concatenate([wide[:, at : at + hd], ones], axis=1)
        win_kv[2 * h + 1] = jnp.concatenate([wide[:, at + hd : at + 2 * hd], zeros], axis=1)
    last_start = jnp.int32(0)
    for r in range(starts_ref.shape[0]):
        last_start = jnp.maximum(
            last_start, jnp.where(starts_ref[r] <= anchor + rows - 1, starts_ref[r], 0)
        )
    token = lax.broadcasted_iota(jnp.int32, (1, rows), 1)
    keep = jnp.where(token >= last_start - anchor, 1.0, 0.0)
    for h in range(heads):
        at = slice(h * padded, (h + 1) * padded)
        channel = (
            lax.broadcasted_iota(jnp.int32, (padded, 2 * channels), 1) % channels
        ).astype(f32)
        one = jnp.where(channel == tab_col[at, 2:3], 1.0, 0.0).astype(bf16)
        two = jnp.where(channel == tab_col[at, 3:4], 1.0, 0.0).astype(bf16)
        left = jnp.dot(one, both_t, preferred_element_type=f32) + tab_col[at, 4:5]
        right = jnp.dot(two, both_t, preferred_element_type=f32) + tab_col[at, 5:6]
        phi_t = (left * right * tab_col[at, 6:7] * keep).astype(bf16)
        own = jnp.dot(phi_t, lin_vals[h], preferred_element_type=f32)
        parts[h * per_head : (h + 1) * per_head] = split_norm(own, hd).reshape(
            per_head, CHUNK, LANES
        )
    for lo in range(0, w_window.shape[1], 256):
        up = min(lo + 256, w_window.shape[1])
        wide[:, lo:up] = jnp.dot(
            normed[...], w_window[:, lo:up], preferred_element_type=f32
        ).astype(bf16)
    for h in range(heads):
        at = 2 * h * hd
        win_q[h] = jnp.concatenate([wide[:, at : at + hd], zeros], axis=1)
        win_kv[2 * h] = jnp.concatenate([wide[:, at + hd : at + 2 * hd], zeros], axis=1)


def attend_body(
    starts_ref, phi_q, feat, feat_t, lin_vals, win_q, win_kv, base, carried, rim, attended,
    hd, fd,
):
    heads, rows, _ = lin_vals.shape
    span = rim.shape[1]
    per_head = base.shape[0] // heads
    padded = per_head * CHUNK
    blocks = span // KV_CHUNK
    anchor = lax.axis_index("seq") * rows
    tile = 128
    lane = lax.broadcasted_iota(jnp.int32, (tile, LANES), 1)
    for b in range(rows // tile):
        first = b * tile
        begin = start_offsets(starts_ref, anchor, tile, first)
        token = lax.broadcasted_iota(jnp.int32, (tile, 1), 0) + first
        use_carry = jnp.where(begin < 0, 1.0, 0.0)
        seen = first + tile
        key_at = lax.broadcasted_iota(jnp.int32, (tile, seen), 1)
        causal = (key_at <= token) & (key_at >= begin)
        slot = lax.broadcasted_iota(jnp.int32, (tile, 2 * span + tile), 1)
        local = slot + (first - 2 * span)
        early = (slot < span) & (slot >= token - begin + 1)
        band = (slot >= span) & (local <= token) & (local > token - span) & (local >= begin)
        visible = early | band
        at = slice(first, first + tile)
        for h in range(heads):
            q = feat[at, h * 2 * fd : h * 2 * fd + fd]
            k_t = feat_t[h * 2 * fd + fd : (h + 1) * 2 * fd, 0:seen]
            similar = jnp.dot(q, k_t, preferred_element_type=f32) * (1.0 / math.sqrt(fd))
            kernel = jnp.where(causal, 1.0 + similar + 0.5 * similar * similar, 0.0)
            mixed = jnp.dot(kernel.astype(bf16), lin_vals[h, 0:seen, :], preferred_element_type=f32)
            phi = phi_q[at, h * padded : (h + 1) * padded]
            own = slice(h * per_head, (h + 1) * per_head)
            from_base = base[own, 0:CHUNK, :].reshape(padded, LANES)
            from_carry = carried[own].reshape(padded, LANES)
            mixed = mixed + jnp.dot(phi, from_base, preferred_element_type=f32)
            mixed = mixed + use_carry * jnp.dot(phi, from_carry, preferred_element_type=f32)
            below = mixed[:, hd : hd + 1] + mixed[:, hd + 1 : hd + 2]
            lin_out = jnp.where(lane < hd, mixed / below, 0.0)
            attended[at, 2 * h * LANES : (2 * h + 1) * LANES] = lin_out.astype(bf16)
            sides = []
            for side in range(2):
                i = 2 * h + side
                cached = base[i * blocks : (i + 1) * blocks, CHUNK:, :].reshape(span, LANES)
                if b == 0:
                    sides.append(
                        jnp.concatenate([cached, rim[i], win_kv[i, 0:tile, :]], axis=0)
                    )
                else:
                    sides.append(
                        jnp.concatenate([cached, win_kv[i, first - span : first + tile, :]], axis=0)
                    )
            scores = lax.dot_general(
                win_q[h, at, :], sides[0], (((1,), (1,)), ((), ())), preferred_element_type=f32
            ) * (1.0 / math.sqrt(hd))
            scores = jnp.where(visible, scores, -1e30)
            weights = jnp.exp(scores - jnp.max(scores, axis=1, keepdims=True))
            weights = (weights / jnp.sum(weights, axis=1, keepdims=True)).astype(bf16)
            win_out = jnp.dot(weights, sides[1], preferred_element_type=f32)
            attended[at, (2 * h + 1) * LANES : (2 * h + 2) * LANES] = win_out.astype(bf16)


def exchange_body(
    hd, where_ref, keep_ref, cache, parts, win_kv, base, carried, rim,
    got_cache, got_parts, mine, got_rows, chosen, results,
    out_c, out_p, out_g, out_b, out_r, in_c, in_p, in_g, in_b, in_r, rim_sems,
):
    me, row = lax.axis_index("seq"), lax.axis_index("grp")
    count, rows = got_cache.shape[0], got_rows.shape[0]
    span, length = rim.shape[1], win_kv.shape[1]

    def seq_copy(src, dst, send, recv, peer):
        return pltpu.make_async_remote_copy(
            src_ref=src, dst_ref=dst, send_sem=send, recv_sem=recv,
            device_id={"seq": peer}, device_id_type=MESH,
        )

    def each_peer(do):
        def step(i, carry):
            do(lax.rem(me + i, count))
            return carry

        lax.fori_loop(1, count, step, 0)

    barrier = pltpu.get_barrier_semaphore()
    each_peer(
        lambda peer: pl.semaphore_signal(
            barrier, inc=1, device_id={"seq": peer}, device_id_type=MESH
        )
    )
    for i in range(1, rows):
        pl.semaphore_signal(
            barrier, inc=1, device_id={"grp": lax.rem(row + i, rows)}, device_id_type=MESH
        )
    pl.semaphore_wait(barrier, count + rows - 2)

    def part_to(peer, slot):
        return seq_copy(parts.at[peer], got_parts.at[slot], out_p.at[peer], in_p.at[slot], peer)

    def cache_to(peer, slot):
        return seq_copy(cache.at[peer], got_cache.at[slot], out_c.at[peer], in_c.at[slot], peer)

    def base_to(peer, slot):
        return seq_copy(chosen, base.at[slot], out_b.at[peer], in_b.at[slot], peer)

    def result_to(peer, slot):
        return seq_copy(results.at[peer], carried.at[slot], out_r.at[peer], in_r.at[slot], peer)

    def row_to(peer, slot):
        return pltpu.make_async_remote_copy(
            src_ref=mine, dst_ref=got_rows.at[slot], send_sem=out_g.at[peer],
            recv_sem=in_g.at[slot], device_id={"grp": peer}, device_id_type=MESH,
        )

    rim_copy = seq_copy(
        win_kv.at[:, pl.ds(length - span, span), :], rim, rim_sems.at[0], rim_sems.at[1],
        lax.rem(me + 1, count),
    )
    each_peer(lambda peer: cache_to(peer, me).start())
    each_peer(lambda peer: part_to(peer, me).start())
    rim_copy.start()
    got_cache[me] = cache[me]
    got_parts[me] = parts[me]
    each_peer(lambda peer: cache_to(peer, peer).wait_recv())
    mine[...] = got_cache[where_ref[0]]
    for i in range(1, rows):
        row_to(lax.rem(row + i, rows), row).start()
    got_rows[row] = mine[...]
    each_peer(lambda peer: part_to(peer, peer).wait_recv())

    def scan(k, total):
        results[k] = split_norm(total, hd)
        return total * keep_ref[k] + got_parts[k].astype(f32)

    lax.fori_loop(0, count, scan, jnp.zeros(parts.shape[1:], f32))
    each_peer(lambda peer: result_to(peer, me).start())
    carried[me] = results[me]
    for i in range(1, rows):
        row_to(lax.rem(row + i, rows), lax.rem(row + i, rows)).wait_recv()
    chosen[...] = got_rows[where_ref[1]]
    each_peer(lambda peer: base_to(peer, me).start())
    base[me] = chosen[...]
    each_peer(lambda peer: result_to(peer, peer).wait_recv())
    each_peer(lambda peer: base_to(peer, peer).wait_recv())
    rim_copy.wait()
    each_peer(lambda peer: cache_to(peer, me).wait_send())
    each_peer(lambda peer: part_to(peer, me).wait_send())
    each_peer(lambda peer: result_to(peer, me).wait_send())
    each_peer(lambda peer: base_to(peer, me).wait_send())
    for i in range(1, rows):
        row_to(lax.rem(row + i, rows), row).wait_send()


def output_body(attended, w_out, out, w_own, w_other, from_other, own_sem, w_send, w_recv, sems):
    me = lax.axis_index("tp")
    other = 1 - me
    half = out.shape[1]
    pieces = w_own.shape[0] // LANES
    hd = w_out.shape[0] // pieces

    def columns(which):
        return pl.ds(pl.multiple_of(which * half, LANES), half)

    barrier = pltpu.get_barrier_semaphore()
    pl.semaphore_signal(barrier, inc=1, device_id={"tp": other}, device_id_type=MESH)
    own, sent = [], []
    for i in range(pieces):
        rows, padded = slice(i * hd, (i + 1) * hd), slice(i * LANES, i * LANES + hd)
        own.append(
            pltpu.make_async_copy(
                w_out.at[rows, columns(me)], w_own.at[padded, :], own_sem.at[i]
            )
        )
        sent.append(
            pltpu.make_async_remote_copy(
                src_ref=w_out.at[rows, columns(other)], dst_ref=w_other.at[padded, :],
                send_sem=w_send.at[i], recv_sem=w_recv.at[i],
                device_id={"tp": other}, device_id_type=MESH,
            )
        )
        own[i].start()
        rest = slice(i * LANES + hd, (i + 1) * LANES)
        w_own[rest, :] = jnp.zeros((LANES - hd, half), bf16)
        w_other[rest, :] = jnp.zeros((LANES - hd, half), bf16)
    pl.semaphore_wait(barrier, 1)
    across = pltpu.make_async_remote_copy(
        src_ref=attended, dst_ref=from_other, send_sem=sems.at[0], recv_sem=sems.at[1],
        device_id={"tp": other}, device_id_type=MESH,
    )
    across.start()
    for copy in sent:
        copy.start()
    for copy in own:
        copy.wait()
    for lo in range(0, half, 256):
        up = min(lo + 256, half)
        out[:, lo:up] = jnp.dot(attended[...], w_own[:, lo:up], preferred_element_type=f32)
    for copy in sent:
        copy.wait()
    across.wait()
    for lo in range(0, half, 256):
        up = min(lo + 256, half)
        out[:, lo:up] += jnp.dot(from_other[...], w_other[:, lo:up], preferred_element_type=f32)


def local(
    hidden_in, norm_gain, w_feature, w_value, w_window, w_out,
    prefix_state, prefix_norm, prefix_kv, lengths, prefix_owner, row_group,
):
    heads, nf, hd = prefix_state.shape[2:]
    fd = w_feature.shape[1] // (2 * heads)
    rows, width = hidden_in.shape[1:]
    span = prefix_kv.shape[2]
    count, groups = lax.axis_size("seq"), lax.axis_size("grp")
    padded = count * CHUNK // heads
    grp = lax.axis_index("grp")
    row = lengths[0]
    starts = jnp.cumsum(row) - row
    first = jnp.arange(count, dtype=jnp.int32)[:, None] * rows
    fresh = jnp.any((starts[None, :] >= first) & (starts[None, :] < first + rows), axis=1)
    keep = 1.0 - fresh.astype(f32)
    where = jnp.stack([prefix_owner[grp], row_group[grp]])
    tab = feature_tables(heads, fd, padded)

    def shape(dims, dtype=bf16):
        return jax.ShapeDtypeStruct(dims, dtype)

    vmem = pl.BlockSpec(memory_space=pltpu.VMEM)
    smem = pl.BlockSpec(memory_space=pltpu.SMEM)
    dma = pltpu.SemaphoreType.DMA
    limit = 60 * 1024 * 1024
    phi_q, feat, feat_t, lin_vals, win_q, win_kv, cache, parts = pl.pallas_call(
        project_body,
        out_shape=[
            shape((rows, heads * padded)),
            shape((rows, 2 * heads * fd)),
            shape((2 * heads * fd, rows)),
            shape((heads, rows, LANES)),
            shape((heads, rows, LANES)),
            shape((2 * heads, rows, LANES)),
            shape((count, CHUNK + KV_CHUNK, LANES)),
            shape((count, CHUNK, LANES)),
        ],
        in_specs=[smem] + [vmem] * 10,
        out_specs=[vmem] * 8,
        scratch_shapes=[pltpu.VMEM((rows, width), bf16), pltpu.VMEM((rows, 2 * heads * hd), bf16)],
        compiler_params=pltpu.CompilerParams(vmem_limit_bytes=limit),
        name="project",
    )(
        starts, hidden_in[0], norm_gain[None], w_feature, w_value, w_window,
        prefix_state[0, 0], prefix_norm[0, 0][:, :, None], prefix_kv[0, 0],
        jnp.asarray(tab), jnp.asarray(np.ascontiguousarray(tab.T)),
    )
    both = CHUNK + KV_CHUNK
    base, carried, rim = pl.pallas_call(
        functools.partial(exchange_body, hd),
        out_shape=[
            shape((count, both, LANES)),
            shape((count, CHUNK, LANES)),
            shape((2 * heads, span, LANES)),
        ],
        in_specs=[smem] * 2 + [vmem] * 3,
        out_specs=[vmem] * 3,
        scratch_shapes=[
            pltpu.VMEM((count, both, LANES), bf16),
            pltpu.VMEM((count, CHUNK, LANES), bf16),
            pltpu.VMEM((both, LANES), bf16),
            pltpu.VMEM((groups, both, LANES), bf16),
            pltpu.VMEM((both, LANES), bf16),
            pltpu.VMEM((count, CHUNK, LANES), bf16),
        ]
        + [dma((count,)), dma((count,)), dma((groups,)), dma((count,)), dma((count,))] * 2
        + [dma((2,))],
        compiler_params=pltpu.CompilerParams(
            collective_id=0, has_side_effects=True, vmem_limit_bytes=limit
        ),
        name="exchange",
    )(where, keep, cache, parts, win_kv)
    attended = pl.pallas_call(
        functools.partial(attend_body, hd=hd, fd=fd),
        out_shape=shape((rows, 2 * heads * LANES)),
        in_specs=[smem] + [vmem] * 9,
        out_specs=vmem,
        compiler_params=pltpu.CompilerParams(vmem_limit_bytes=limit),
        name="attend",
    )(starts, phi_q, feat, feat_t, lin_vals, win_q, win_kv, base, carried, rim)
    columns = width // lax.axis_size("tp")
    mixed = pl.pallas_call(
        output_body,
        out_shape=shape((rows, columns), f32),
        in_specs=[vmem] * 2,
        out_specs=vmem,
        scratch_shapes=[
            pltpu.VMEM((2 * heads * LANES, columns), bf16),
            pltpu.VMEM((2 * heads * LANES, columns), bf16),
            pltpu.VMEM((rows, 2 * heads * LANES), bf16),
            dma((2 * heads,)), dma((2 * heads,)), dma((2 * heads,)), dma((2,)),
        ],
        compiler_params=pltpu.CompilerParams(
            collective_id=1, has_side_effects=True, vmem_limit_bytes=limit
        ),
        name="mix",
    )(attended, w_out)
    at = lax.axis_index("tp") * columns
    residual = lax.dynamic_slice_in_dim(hidden_in[0], at, columns, 1).astype(f32)
    return (residual + mixed)[None]


def solution(mesh):
    placed = (
        P("grp", "seq", None),
        P(),
        P(None, "tp"),
        P(None, "tp"),
        P(None, "tp"),
        P("tp", None),
        P("grp", "seq", "tp", None, None),
        P("grp", "seq", "tp", None),
        P("grp", "seq", None, "tp"),
        P("grp", None),
        P(),
        P(),
    )
    return jax.shard_map(
        local, mesh=mesh, in_specs=placed, out_specs=P("grp", "seq", "tp"), check_vma=False
    )
```

```python
import functools
import math

import jax
import jax.numpy as jnp
import numpy as np
from jax import lax
from jax.experimental import pallas as pl
from jax.experimental.pallas import tpu as pltpu
from jax.sharding import PartitionSpec as P

MESH = pl.DeviceIdType.MESH
LANES = 128
NEAR = 4
CHUNK = 32
HIGH = 20
KV_CHUNK = 16
f32, bf16 = jnp.float32, jnp.bfloat16


def feature_tables(fd, chunks):
    first, second = np.triu_indices(fd)
    pair = 1 + fd + np.arange(len(first))
    order = np.concatenate(
        [[0], pair[first == second], 1 + np.arange(fd), pair[first != second]]
    ).astype(np.int64)
    rows = np.zeros((8, chunks * CHUNK), np.float32)
    rows[0:4] = -1.0
    rows[7] = -1.0
    for rank, feature in enumerate(order):
        chunk, at = rank % chunks, rank // chunks
        spots = [chunk * CHUNK + at]
        if at < CHUNK - HIGH:
            spots.append(chunk * CHUNK + HIGH + at)
        for spot in spots:
            rows[7, spot] = feature
            if feature == 0:
                rows[4:7, spot] = 1.0
            elif feature <= fd:
                rows[0, spot], rows[2, spot] = feature - 1, fd + feature - 1
                rows[5, spot], rows[6, spot] = 1.0, 1.0 / fd**0.25
            else:
                i, j = first[feature - 1 - fd], second[feature - 1 - fd]
                rows[0, spot], rows[1, spot] = i, j
                rows[2, spot], rows[3, spot] = fd + i, fd + j
                rows[6, spot] = 1.0 / math.sqrt(2.0 * fd if i == j else fd)
    return rows


def halves(x):
    hi = x.astype(bf16)
    return hi, (x - hi.astype(f32)).astype(bf16)


def dropped(x):
    return x - x.astype(bf16).astype(f32)


def places_of(shape):
    lane = lax.broadcasted_iota(jnp.int32, shape, 1)
    low = lax.broadcasted_iota(jnp.int32, shape, 0) % CHUNK >= HIGH
    return lane, low


def pack_new(x, hd):
    lane, low = places_of(x.shape)
    lost = dropped(x)
    high_rows = jnp.where(lane == hd + 1, pltpu.roll(lost, 1, 1), x)
    low_rows = jnp.where(lane < hd, lost, 0.0)
    return jnp.where(low, low_rows, high_rows).astype(bf16)


def pack_sum(x, hd):
    lane, low = places_of(x.shape)
    lost = dropped(x)
    x = jnp.where((lane == hd + 1) & ~low, x + pltpu.roll(lost, 1, 1), x)
    return jnp.where((lane < hd) & low, x + pltpu.roll(lost, HIGH, 0), x).astype(bf16)


def kernel(
    sizes,
    lengths, owners, groups, hidden_hbm, gain, w_feature, w_value_hbm, w_window_hbm, w_out,
    state, norm, kv, tab_row, tab_col,
    out,
    hidden, w_value, w_window, normed, wide, phi_q, feat, feat_t, lin_vals, win_q, win_kv, intra,
    cache, parts, got_near, quarter, got_far, mine, got_rows, base, got_parts, results, carried,
    rim, attended, from_other, w_own, w_other,
    load_sems, own_sems, w_send, w_recv, a_send, a_recv,
    near_out, near_in, far_out, far_in, row_out, row_in, bfar_out, bfar_in, bnear_out, bnear_in,
    part_out, part_in, res_out, res_in, rim_sems,
):
    heads, nf, hd, fd, count = sizes
    rows, width = hidden.shape
    span = rim.shape[1]
    half = out.shape[1]
    chunks = count // heads
    padded = chunks * CHUNK
    blocks = span // KV_CHUNK
    far = count // NEAR
    grp_count = got_rows.shape[0]
    row, me, core = lax.axis_index("grp"), lax.axis_index("seq"), lax.axis_index("tp")
    my_far, my_near = me // NEAR, me % NEAR
    other = 1 - core
    anchor = me * rows

    def remote(src, dst, send, recv, where):
        return pltpu.make_async_remote_copy(
            src_ref=src, dst_ref=dst, send_sem=send, recv_sem=recv,
            device_id=where, device_id_type=MESH,
        )

    def each_seq(do):
        def step(i, carry):
            off = count // 2 + ((i + 1) // 2) * (2 * (i % 2) - 1)
            do(lax.rem(me + off, count))
            return carry

        lax.fori_loop(0, count - 1, step, 0)

    def each_near(do):
        for i in (2, 1, 3):
            do(lax.rem(my_near + i, NEAR))

    def each_far(do):
        for i in (4, 3, 5, 2, 6, 1, 7):
            do(lax.rem(my_far + i, far))

    def each_row(do):
        for i in (2, 1, 3):
            do(lax.rem(row + i, grp_count))

    def near_copy(peer, slot):
        return remote(
            cache.at[pl.ds(peer * far, far)], got_near.at[slot], near_out.at[peer],
            near_in.at[slot], {"seq": my_far * NEAR + peer},
        )

    def far_copy(peer, slot):
        return remote(
            quarter.at[peer], got_far.at[slot], far_out.at[peer], far_in.at[slot],
            {"seq": peer * NEAR + my_near},
        )

    def row_copy(peer, slot):
        return remote(
            mine, got_rows.at[slot], row_out.at[peer], row_in.at[slot], {"grp": peer}
        )

    def base_far_copy(peer, slot):
        return remote(
            base.at[my_near * far + my_far], base.at[my_near * far + slot], bfar_out.at[peer],
            bfar_in.at[slot], {"seq": peer * NEAR + my_near},
        )

    def base_near_copy(peer, slot):
        return remote(
            base.at[pl.ds(my_near * far, far)], base.at[pl.ds(slot * far, far)],
            bnear_out.at[peer], bnear_in.at[slot], {"seq": my_far * NEAR + peer},
        )

    def part_copy(peer, slot):
        return remote(
            parts.at[peer], got_parts.at[slot], part_out.at[peer], part_in.at[slot],
            {"seq": peer},
        )

    def result_copy(peer, slot):
        return remote(
            results.at[peer], carried.at[slot], res_out.at[peer], res_in.at[slot],
            {"seq": peer},
        )

    def columns(which):
        return pl.ds(pl.multiple_of(which * half, LANES), half)

    loads = [
        pltpu.make_async_copy(hidden_hbm, hidden, load_sems.at[0]),
        pltpu.make_async_copy(w_value_hbm, w_value, load_sems.at[1]),
        pltpu.make_async_copy(w_window_hbm, w_window, load_sems.at[2]),
    ]
    for load in loads:
        load.start()
    own_w, sent_w, across = [], [], []
    for i in range(2 * heads):
        src, dst = slice(i * hd, (i + 1) * hd), slice(i * LANES, i * LANES + hd)
        own_w.append(
            pltpu.make_async_copy(w_out.at[src, columns(core)], w_own.at[dst, :], own_sems.at[i])
        )
        sent_w.append(
            remote(
                w_out.at[src, columns(other)], w_other.at[dst, :], w_send.at[i], w_recv.at[i],
                {"tp": other},
            )
        )
        tile = slice(i * LANES, (i + 1) * LANES)
        across.append(
            remote(
                attended.at[:, tile], from_other.at[:, tile], a_send.at[i], a_recv.at[i],
                {"tp": other},
            )
        )
    rim_copy = remote(
        win_kv.at[:, pl.ds(rows - span, span), :], rim, rim_sems.at[0], rim_sems.at[1],
        {"seq": lax.rem(me + 1, count)},
    )

    barrier = pltpu.get_barrier_semaphore()

    def greet(where):
        pl.semaphore_signal(barrier, inc=1, device_id=where, device_id_type=MESH)

    each_seq(lambda peer: greet({"seq": peer}))
    each_row(lambda peer: greet({"grp": peer}))
    greet({"tp": other})

    starts, total = [], jnp.int32(0)
    for r in range(lengths.shape[1]):
        starts.append(total)
        total = total + lengths[0, r]

    def start_of(place):
        best = jnp.int32(0)
        for start in starts:
            best = jnp.maximum(best, jnp.where(start <= place, start, 0))
        return best

    pick = jnp.where(
        lax.broadcasted_iota(jnp.int32, (padded, nf), 1).astype(f32) == tab_col[:, 7:8], 1.0, 0.0
    ).astype(bf16)
    norm_hi, norm_lo = halves(norm[...])
    contract = (((1,), (1,)), ((), ()))
    norms = lax.dot_general(pick, norm_hi, contract, preferred_element_type=f32)
    norms = norms + lax.dot_general(pick, norm_lo, contract, preferred_element_type=f32)
    for h in range(heads):
        hi, lo = halves(state[h])
        body = jnp.dot(pick, hi, preferred_element_type=f32)
        body = body + jnp.dot(pick, lo, preferred_element_type=f32)
        body = jnp.concatenate(
            [body, norms[:, h : h + 1], jnp.zeros((padded, LANES - hd - 1), f32)], axis=1
        )
        cache[h * chunks : (h + 1) * chunks, 0:CHUNK, :] = pack_new(body, hd).reshape(
            chunks, CHUNK, LANES
        )
    for i in range(2 * heads):
        piece = jnp.concatenate(
            [kv[:, i * hd : (i + 1) * hd], jnp.zeros((span, LANES - hd), bf16)], axis=1
        )
        cache[i * blocks : (i + 1) * blocks, CHUNK:, :] = piece.reshape(blocks, KV_CHUNK, LANES)
    for copy in own_w:
        copy.start()
    for i in range(2 * heads):
        rest = slice(i * LANES + hd, (i + 1) * LANES)
        w_own[rest, :] = jnp.zeros((LANES - hd, half), bf16)
        w_other[rest, :] = jnp.zeros((LANES - hd, half), bf16)

    loads[0].wait()
    step = 64
    scale = gain[...].reshape(1, width)

    def norm_rows(i, carry):
        at = pl.ds(pl.multiple_of(i * step, step), step)
        x = hidden[at, :].astype(f32)
        inv = lax.rsqrt(jnp.mean(x * x, axis=1, keepdims=True) + 1e-5)
        normed[at, :] = (x * inv * scale).astype(bf16)
        return carry

    lax.fori_loop(0, rows // step, norm_rows, 0)

    pl.semaphore_wait(barrier, count - 1 + grp_count - 1 + 1)
    each_near(lambda peer: near_copy(peer, my_near).start())
    got_near[my_near] = cache[pl.ds(my_near * far, far)]

    feats = jnp.dot(normed[...], w_feature[...], preferred_element_type=f32)
    both_t = jnp.concatenate(halves(jnp.transpose(feats)), axis=0)
    both = jnp.concatenate(halves(feats), axis=1)
    channels = feats.shape[1]
    feat[...] = both[:, 0:channels]
    feat_t[...] = both_t[0:channels, :]
    loads[1].wait()
    for lo in range(0, w_value.shape[1], 256):
        up = min(lo + 256, w_value.shape[1])
        wide[:, lo:up] = jnp.dot(
            normed[...], w_value[:, lo:up], preferred_element_type=f32
        ).astype(bf16)
    lane = lax.broadcasted_iota(jnp.int32, (rows, LANES - hd), 1)
    ones = jnp.where(lane == 0, 1.0, 0.0).astype(bf16)
    zeros = jnp.zeros((rows, LANES - hd), bf16)
    for h in range(heads):
        at = 2 * h * hd
        lin_vals[h] = jnp.concatenate([wide[:, at : at + hd], ones], axis=1)
    token = lax.broadcasted_iota(jnp.int32, (1, rows), 1)
    keep = jnp.where(token >= start_of(anchor + rows - 1) - anchor, 1.0, 0.0)
    for h in range(heads):
        channel = (
            lax.broadcasted_iota(jnp.int32, (padded, 2 * channels), 1) % channels - h * 2 * fd
        ).astype(f32)
        one = jnp.where((channel == tab_col[:, 2:3]) & (channel >= 0.0), 1.0, 0.0).astype(bf16)
        two = jnp.where((channel == tab_col[:, 3:4]) & (channel >= 0.0), 1.0, 0.0).astype(bf16)
        left = jnp.dot(one, both_t, preferred_element_type=f32) + tab_col[:, 4:5]
        right = jnp.dot(two, both_t, preferred_element_type=f32) + tab_col[:, 5:6]
        phi_t = (left * right * tab_col[:, 6:7] * keep).astype(bf16)
        own = jnp.dot(phi_t, lin_vals[h], preferred_element_type=f32)
        parts[h * chunks : (h + 1) * chunks] = pack_new(own, hd).reshape(chunks, CHUNK, LANES)
    each_seq(lambda peer: part_copy(peer, me).start())
    got_parts[me] = parts[me]

    owner = owners[row]
    each_near(lambda peer: near_copy(peer, peer).wait_recv())
    quarter[...] = got_near[owner % NEAR]
    each_far(lambda peer: far_copy(peer, my_far).start())
    got_far[my_far] = quarter[my_far]
    for copy in sent_w:
        copy.start()

    for h in range(heads):
        at = 2 * h * hd
        win_kv[2 * h + 1] = jnp.concatenate([wide[:, at + hd : at + 2 * hd], zeros], axis=1)
    loads[2].wait()
    for lo in range(0, w_window.shape[1], 256):
        up = min(lo + 256, w_window.shape[1])
        wide[:, lo:up] = jnp.dot(
            normed[...], w_window[:, lo:up], preferred_element_type=f32
        ).astype(bf16)
    for h in range(heads):
        at = 2 * h * hd
        win_q[h] = jnp.concatenate([wide[:, at : at + hd], zeros], axis=1)
        win_kv[2 * h] = jnp.concatenate([wide[:, at + hd : at + 2 * hd], zeros], axis=1)
    rim_copy.start()

    each_far(lambda peer: far_copy(peer, peer).wait_recv())
    mine[...] = got_far[owner // NEAR]
    each_row(lambda peer: row_copy(peer, row).start())
    got_rows[row] = mine[...]

    for h in range(heads):
        channel = (
            lax.broadcasted_iota(jnp.int32, (2 * channels, padded), 0) % channels - h * 2 * fd
        ).astype(f32)
        one = jnp.where((channel == tab_row[0:1, :]) & (channel >= 0.0), 1.0, 0.0).astype(bf16)
        two = jnp.where((channel == tab_row[1:2, :]) & (channel >= 0.0), 1.0, 0.0).astype(bf16)
        left = jnp.dot(both, one, preferred_element_type=f32) + tab_row[4:5, :]
        right = jnp.dot(both, two, preferred_element_type=f32) + tab_row[5:6, :]
        phi_q[:, h * padded : (h + 1) * padded] = (left * right * tab_row[6:7, :]).astype(bf16)

    each_row(lambda peer: row_copy(peer, peer).wait_recv())
    base[my_near * far + my_far] = got_rows[groups[row]]
    each_far(lambda peer: base_far_copy(peer, my_far).start())

    tile = 128
    begins = []
    for b in range(rows // tile):
        place = lax.broadcasted_iota(jnp.int32, (tile, 1), 0) + (b * tile + anchor)
        best = jnp.zeros((tile, 1), jnp.int32)
        for start in starts:
            best = jnp.maximum(best, jnp.where(start <= place, start, 0))
        begins.append(best - anchor)

    def within(b):
        first, seen = b * tile, (b + 1) * tile
        tokens = lax.broadcasted_iota(jnp.int32, (tile, 1), 0) + first
        key_at = lax.broadcasted_iota(jnp.int32, (tile, seen), 1)
        causal = (key_at <= tokens) & (key_at >= begins[b])
        for h in range(heads):
            q = feat[first:seen, h * 2 * fd : h * 2 * fd + fd]
            k_t = feat_t[h * 2 * fd + fd : (h + 1) * 2 * fd, 0:seen]
            similar = jnp.dot(q, k_t, preferred_element_type=f32) * (1.0 / math.sqrt(fd))
            mass = jnp.where(causal, 1.0 + similar + 0.5 * similar * similar, 0.0)
            intra[h, first:seen, :] = jnp.dot(
                mass.astype(bf16), lin_vals[h, 0:seen, :], preferred_element_type=f32
            )

    within(3)

    each_seq(lambda peer: part_copy(peer, peer).wait_recv())

    def scan(k, carry):
        results[k] = pack_sum(carry, hd)
        restart = start_of(k * rows + rows - 1) >= k * rows
        return carry * jnp.where(restart, 0.0, 1.0) + got_parts[k].astype(f32)

    lax.fori_loop(0, count, scan, jnp.zeros((CHUNK, LANES), f32))
    each_seq(lambda peer: result_copy(peer, me).start())
    carried[me] = results[me]

    each_far(lambda peer: base_far_copy(peer, peer).wait_recv())
    each_near(lambda peer: base_near_copy(peer, my_near).start())
    for b in range(3):
        within(b)

    each_near(lambda peer: base_near_copy(peer, peer).wait_recv())
    rim_copy.wait()
    for h in range(heads):
        for b in range(rows // tile):
            first = b * tile
            tokens = lax.broadcasted_iota(jnp.int32, (tile, 1), 0) + first
            slot = lax.broadcasted_iota(jnp.int32, (tile, 2 * span + tile), 1)
            near_at = slot + (first - 2 * span)
            early = (slot < span) & (slot >= tokens - begins[b] + 1)
            band = (
                (slot >= span) & (near_at <= tokens) & (near_at > tokens - span)
                & (near_at >= begins[b])
            )
            sides = []
            for i in (2 * h, 2 * h + 1):
                cached = base[i * blocks : (i + 1) * blocks, CHUNK:, :].reshape(span, LANES)
                if b == 0:
                    recent = [rim[i], win_kv[i, 0:tile, :]]
                else:
                    recent = [win_kv[i, first - span : first + tile, :]]
                sides.append(jnp.concatenate([cached] + recent, axis=0))
            scores = lax.dot_general(
                win_q[h, first : first + tile, :], sides[0], contract, preferred_element_type=f32
            ) * (1.0 / math.sqrt(hd))
            scores = jnp.where(early | band, scores, -1e30)
            weights = jnp.exp(scores - jnp.max(scores, axis=1, keepdims=True))
            weights = (weights / jnp.sum(weights, axis=1, keepdims=True)).astype(bf16)
            win_out = jnp.dot(weights, sides[1], preferred_element_type=f32)
            attended[first : first + tile, (2 * h + 1) * LANES : (2 * h + 2) * LANES] = (
                win_out.astype(bf16)
            )
        across[2 * h + 1].start()

    each_seq(lambda peer: result_copy(peer, peer).wait_recv())
    for h in range(heads):
        own = slice(h * chunks, (h + 1) * chunks)
        from_base = base[own, 0:CHUNK, :].reshape(padded, LANES)
        from_carry = carried[own].reshape(padded, LANES)
        for b in range(rows // tile):
            at = slice(b * tile, (b + 1) * tile)
            use_carry = jnp.where(begins[b] < 0, 1.0, 0.0)
            phi = phi_q[at, h * padded : (h + 1) * padded]
            mixed = intra[h, at, :] + jnp.dot(phi, from_base, preferred_element_type=f32)
            mixed = mixed + use_carry * jnp.dot(phi, from_carry, preferred_element_type=f32)
            below = mixed[:, hd : hd + 1] + mixed[:, hd + 1 : hd + 2]
            lane = lax.broadcasted_iota(jnp.int32, (tile, LANES), 1)
            attended[at, 2 * h * LANES : (2 * h + 1) * LANES] = jnp.where(
                lane < hd, mixed / below, 0.0
            ).astype(bf16)
        across[2 * h].start()

    for copy in own_w:
        copy.wait()
    for lo in range(0, half, 256):
        up = min(lo + 256, half)
        out[:, lo:up] = jnp.dot(attended[...], w_own[:, lo:up], preferred_element_type=f32)
    for copy in sent_w:
        copy.wait()
    for copy in across:
        copy.wait()
    for lo in range(0, half, 256):
        up = min(lo + 256, half)
        out[:, lo:up] += jnp.dot(from_other[...], w_other[:, lo:up], preferred_element_type=f32)
    each_near(lambda peer: near_copy(peer, my_near).wait_send())
    each_far(lambda peer: far_copy(peer, my_far).wait_send())
    each_row(lambda peer: row_copy(peer, row).wait_send())
    each_far(lambda peer: base_far_copy(peer, my_far).wait_send())
    each_near(lambda peer: base_near_copy(peer, my_near).wait_send())
    each_seq(lambda peer: part_copy(peer, me).wait_send())
    each_seq(lambda peer: result_copy(peer, me).wait_send())


def local(
    hidden_in, norm_gain, w_feature, w_value, w_window, w_out,
    prefix_state, prefix_norm, prefix_kv, lengths, prefix_owner, row_group,
):
    heads, nf, hd = prefix_state.shape[2:]
    fd = w_feature.shape[1] // (2 * heads)
    rows, width = hidden_in.shape[1:]
    span = prefix_kv.shape[2]
    count, groups = lax.axis_size("seq"), lax.axis_size("grp")
    far = count // NEAR
    chunks = count // heads
    columns = width // lax.axis_size("tp")
    tab = feature_tables(fd, chunks)
    both = CHUNK + KV_CHUNK
    dma = pltpu.SemaphoreType.DMA

    def pair(n):
        return [dma((n,)), dma((n,))]

    def vm(*dims, dtype=bf16):
        return pltpu.VMEM(dims, dtype)

    vmem = pl.BlockSpec(memory_space=pltpu.VMEM)
    smem = pl.BlockSpec(memory_space=pltpu.SMEM)
    anywhere = pl.BlockSpec(memory_space=pl.ANY)
    mixed = pl.pallas_call(
        functools.partial(kernel, (heads, nf, hd, fd, count)),
        out_shape=jax.ShapeDtypeStruct((rows, columns), f32),
        in_specs=[smem] * 3
        + [anywhere, vmem, vmem, anywhere, anywhere, anywhere]
        + [vmem] * 5,
        out_specs=vmem,
        scratch_shapes=[
            vm(rows, width), vm(width, 2 * heads * hd), vm(width, 2 * heads * hd),
            vm(rows, width), vm(rows, 2 * heads * hd),
            vm(rows, heads * chunks * CHUNK), vm(rows, 2 * heads * fd), vm(2 * heads * fd, rows),
            vm(heads, rows, LANES), vm(heads, rows, LANES), vm(2 * heads, rows, LANES),
            vm(heads, rows, LANES, dtype=f32),
            vm(count, both, LANES), vm(count, CHUNK, LANES),
            vm(NEAR, far, both, LANES), vm(far, both, LANES), vm(far, both, LANES),
            vm(both, LANES), vm(groups, both, LANES), vm(count, both, LANES),
            vm(count, CHUNK, LANES), vm(count, CHUNK, LANES), vm(count, CHUNK, LANES),
            vm(2 * heads, span, LANES),
            vm(rows, 2 * heads * LANES), vm(rows, 2 * heads * LANES),
            vm(2 * heads * LANES, columns), vm(2 * heads * LANES, columns),
            dma((3,)), dma((2 * heads,)),
        ]
        + pair(2 * heads) + pair(2 * heads)
        + pair(NEAR) + pair(far) + pair(groups) + pair(far) + pair(NEAR)
        + pair(count) + pair(count) + [dma((2,))],
        compiler_params=pltpu.CompilerParams(
            collective_id=0, has_side_effects=True, vmem_limit_bytes=60 * 1024 * 1024
        ),
        name="mixers",
    )(
        lengths, prefix_owner, row_group,
        hidden_in[0], norm_gain, w_feature, w_value, w_window, w_out,
        prefix_state[0, 0], prefix_norm[0, 0], prefix_kv[0, 0],
        jnp.asarray(tab), jnp.asarray(np.ascontiguousarray(tab.T)),
    )
    at = lax.axis_index("tp") * columns
    residual = lax.dynamic_slice_in_dim(hidden_in[0], at, columns, 1).astype(f32)
    return (residual + mixed)[None]


def solution(mesh):
    placed = (
        P("grp", "seq", None),
        P(),
        P(None, "tp"),
        P(None, "tp"),
        P(None, "tp"),
        P("tp", None),
        P("grp", "seq", "tp", None, None),
        P("grp", "seq", "tp", None),
        P("grp", "seq", None, "tp"),
        P("grp", None),
        P(),
        P(),
    )
    return jax.shard_map(
        local, mesh=mesh, in_specs=placed, out_specs=P("grp", "seq", "tp"), check_vma=False
    )
```

```python
import functools
import math

import jax
import jax.numpy as jnp
import numpy as np
from jax import lax
from jax.experimental import pallas as pl
from jax.experimental.pallas import tpu as pltpu
from jax.sharding import PartitionSpec as P

MESH = pl.DeviceIdType.MESH
LANES = 128
NEAR = 4
CHUNK = 24
HIGH = 20
KV_CHUNK = 16
f32, bf16 = jnp.float32, jnp.bfloat16


def feature_tables(fd, chunks):
    first, second = np.triu_indices(fd)
    pair = 1 + fd + np.arange(len(first))
    order = np.concatenate(
        [[0], pair[first == second], 1 + np.arange(fd), pair[first != second]]
    ).astype(np.int64)
    rows = np.zeros((8, chunks * CHUNK), np.float32)
    rows[0:4] = -1.0
    rows[7] = -1.0
    for rank, feature in enumerate(order):
        chunk, at = rank % chunks, rank // chunks
        spots = [chunk * CHUNK + at]
        if at < CHUNK - HIGH:
            spots.append(chunk * CHUNK + HIGH + at)
        for spot in spots:
            rows[7, spot] = feature
            if feature == 0:
                rows[4:7, spot] = 1.0
            elif feature <= fd:
                rows[0, spot], rows[2, spot] = feature - 1, fd + feature - 1
                rows[5, spot], rows[6, spot] = 1.0, 1.0 / fd**0.25
            else:
                i, j = first[feature - 1 - fd], second[feature - 1 - fd]
                rows[0, spot], rows[1, spot] = i, j
                rows[2, spot], rows[3, spot] = fd + i, fd + j
                rows[6, spot] = 1.0 / math.sqrt(2.0 * fd if i == j else fd)
    return rows


def halves(x):
    hi = x.astype(bf16)
    return hi, (x - hi.astype(f32)).astype(bf16)


def dropped(x):
    return x - x.astype(bf16).astype(f32)


def places_of(shape):
    lane = lax.broadcasted_iota(jnp.int32, shape, 1)
    low = lax.broadcasted_iota(jnp.int32, shape, 0) % CHUNK >= HIGH
    return lane, low


def pack_new(x, hd):
    lane, low = places_of(x.shape)
    lost = dropped(x)
    high_rows = jnp.where(lane == hd + 1, pltpu.roll(lost, 1, 1), x)
    low_rows = jnp.where(lane < hd, lost, 0.0)
    return jnp.where(low, low_rows, high_rows).astype(bf16)


def pack_sum(x, hd):
    lane, low = places_of(x.shape)
    lost = dropped(x)
    x = jnp.where((lane == hd + 1) & ~low, x + pltpu.roll(lost, 1, 1), x)
    return jnp.where((lane < hd) & low, x + pltpu.roll(lost, HIGH, 0), x).astype(bf16)


def kernel(
    sizes,
    lengths, owners, groups, hidden_hbm, gain, w_feature_hbm, w_value_hbm, w_window_hbm, w_out,
    state_hbm, norm, kv_hbm, tab_row, tab_col,
    out,
    restarts, state, kv, hidden, w_feature, w_value, w_window, normed, wide, phi_q, feat, feat_t, lin_vals, win_q, win_kv, intra,
    cache, parts, got_near, quarter, got_far, mine, got_rows, base, got_parts, results, carried,
    rim, attended, from_other, w_own, w_other,
    load_sems, own_sems, w_send, w_recv, a_send, a_recv,
    near_out, near_in, far_out, far_in, row_out, row_in, bfar_out, bfar_in, slab_out, slab_in,
    part_out, part_in, res_out, res_in, rim_sems,
):
    heads, nf, hd, fd, count = sizes
    rows, width = hidden.shape
    span = rim.shape[1]
    half = out.shape[1]
    chunks = count // heads
    padded = chunks * CHUNK
    blocks = span // KV_CHUNK
    far = count // NEAR
    grp_count = got_rows.shape[0]
    row, me, core = lax.axis_index("grp"), lax.axis_index("seq"), lax.axis_index("tp")
    my_far, my_near = me // NEAR, me % NEAR
    other = 1 - core
    anchor = me * rows

    def remote(src, dst, send, recv, where):
        return pltpu.make_async_remote_copy(
            src_ref=src, dst_ref=dst, send_sem=send, recv_sem=recv,
            device_id=where, device_id_type=MESH,
        )

    def each_seq(do):
        def step(i, carry):
            off = count // 2 + ((i + 1) // 2) * (2 * (i % 2) - 1)
            do(lax.rem(me + off, count))
            return carry

        lax.fori_loop(0, count - 1, step, 0)

    def each_near(do):
        for i in (2, 1, 3):
            do(lax.rem(my_near + i, NEAR))

    def each_far(do):
        for i in (4, 3, 5, 2, 6, 1, 7):
            do(lax.rem(my_far + i, far))

    def each_row(do):
        for i in (2, 1, 3):
            do(lax.rem(row + i, grp_count))

    def near_copy(peer, slot):
        return remote(
            cache.at[pl.ds(peer * far, far)], got_near.at[slot], near_out.at[peer],
            near_in.at[slot], {"seq": my_far * NEAR + peer},
        )

    def far_copy(peer, slot):
        return remote(
            quarter.at[peer], got_far.at[slot], far_out.at[peer], far_in.at[slot],
            {"seq": peer * NEAR + my_near},
        )

    def row_copy(peer, slot):
        return remote(
            mine, got_rows.at[slot], row_out.at[peer], row_in.at[slot], {"grp": peer}
        )

    def base_far_copy(peer, slot):
        return remote(
            base.at[my_near * far + my_far], base.at[my_near * far + slot], bfar_out.at[peer],
            bfar_in.at[slot], {"seq": peer * NEAR + my_near},
        )

    kinds = (slice(0, KV_CHUNK), slice(KV_CHUNK, KV_CHUNK + CHUNK))
    east, west = lax.rem(my_near + 1, NEAR), lax.rem(my_near + NEAR - 1, NEAR)

    def slab_copies(kind, forward):
        copies = []
        for way, peer in enumerate((east, west)):
            first, size = my_near * far, far
            if forward:
                first, size = (west, east)[way] * far + way * (far // 2), far // 2
            part = base.at[pl.ds(first, size), kinds[kind], :]
            at = 4 * forward + 2 * kind + way
            copies.append(
                remote(
                    part, part, slab_out.at[at], slab_in.at[at], {"seq": my_far * NEAR + peer}
                )
            )
        return copies

    slabs = {(kind, forward): slab_copies(kind, forward) for kind in (0, 1) for forward in (0, 1)}

    def slab_arrived(kind, forward):
        for way in range(2):
            first, size = (west, east)[way] * far, far
            if forward:
                first, size = lax.rem(my_near + 2, NEAR) * far + way * (far // 2), far // 2
            part = base.at[pl.ds(first, size), kinds[kind], :]
            at = 4 * forward + 2 * kind + way
            remote(
                part, part, slab_out.at[at], slab_in.at[at],
                {"seq": my_far * NEAR + (east, west)[way]},
            ).wait_recv()

    def part_copy(peer, slot):
        return remote(
            parts.at[peer], got_parts.at[slot], part_out.at[peer], part_in.at[slot],
            {"seq": peer},
        )

    def result_copy(peer, slot):
        return remote(
            results.at[peer], carried.at[slot], res_out.at[peer], res_in.at[slot],
            {"seq": peer},
        )

    def columns(which):
        return pl.ds(pl.multiple_of(which * half, LANES), half)

    loads = [
        pltpu.make_async_copy(hidden_hbm, hidden, load_sems.at[0]),
        pltpu.make_async_copy(w_feature_hbm, w_feature, load_sems.at[1]),
        pltpu.make_async_copy(w_value_hbm, w_value, load_sems.at[2]),
        pltpu.make_async_copy(kv_hbm, kv, load_sems.at[3]),
    ] + [
        pltpu.make_async_copy(state_hbm.at[:, h, :], state.at[h], load_sems.at[4 + h])
        for h in range(heads)
    ]
    last_load = pltpu.make_async_copy(w_window_hbm, w_window, load_sems.at[4 + heads])
    for load in loads:
        load.start()
    own_w, sent_w, across = [], [], []
    for i in range(2 * heads):
        src, dst = slice(i * hd, (i + 1) * hd), slice(i * LANES, i * LANES + hd)
        own_w.append(
            pltpu.make_async_copy(w_out.at[src, columns(core)], w_own.at[dst, :], own_sems.at[i])
        )
        sent_w.append(
            remote(
                w_out.at[src, columns(other)], w_other.at[dst, :], w_send.at[i], w_recv.at[i],
                {"tp": other},
            )
        )
        tile = slice(i * LANES, (i + 1) * LANES)
        across.append(
            remote(
                attended.at[:, tile], from_other.at[:, tile], a_send.at[i], a_recv.at[i],
                {"tp": other},
            )
        )
    rim_copy = remote(
        win_kv.at[:, pl.ds(rows - span, span), :], rim, rim_sems.at[0], rim_sems.at[1],
        {"seq": lax.rem(me + 1, count)},
    )

    barrier = pltpu.get_barrier_semaphore()

    def greet(where):
        pl.semaphore_signal(barrier, inc=1, device_id=where, device_id_type=MESH)

    each_seq(lambda peer: greet({"seq": peer}))
    each_row(lambda peer: greet({"grp": peer}))
    greet({"tp": other})

    starts, total = [], jnp.int32(0)
    for r in range(lengths.shape[1]):
        starts.append(total)
        total = total + lengths[0, r]

    def start_of(place):
        best = jnp.int32(0)
        for start in starts:
            best = jnp.maximum(best, jnp.where(start <= place, start, 0))
        return best

    def note(k, carry):
        restarts[k] = jnp.where(start_of(k * rows + rows - 1) >= k * rows, 0.0, 1.0)
        return carry

    lax.fori_loop(0, count, note, 0)

    loads[0].wait()
    last_load.start()
    step = 64
    scale = gain[...].reshape(1, width)

    def norm_rows(i, carry):
        at = pl.ds(pl.multiple_of(i * step, step), step)
        x = hidden[at, :].astype(f32)
        inv = lax.rsqrt(jnp.mean(x * x, axis=1, keepdims=True) + 1e-5)
        normed[at, :] = (x * inv * scale).astype(bf16)
        return carry

    lax.fori_loop(0, rows // step, norm_rows, 0)

    pick = jnp.where(
        lax.broadcasted_iota(jnp.int32, (padded, nf), 1).astype(f32) == tab_col[:, 7:8], 1.0, 0.0
    ).astype(bf16)
    for load in loads[3:]:
        load.wait()
    norm_hi, norm_lo = halves(norm[...])
    contract = (((1,), (1,)), ((), ()))
    norms = lax.dot_general(pick, norm_hi, contract, preferred_element_type=f32)
    norms = norms + lax.dot_general(pick, norm_lo, contract, preferred_element_type=f32)
    for h in range(heads):
        hi, lo = halves(state[h])
        body = jnp.dot(pick, hi, preferred_element_type=f32)
        body = body + jnp.dot(pick, lo, preferred_element_type=f32)
        body = jnp.concatenate(
            [body, norms[:, h : h + 1], jnp.zeros((padded, LANES - hd - 1), f32)], axis=1
        )
        cache[h * chunks : (h + 1) * chunks, KV_CHUNK:, :] = pack_new(body, hd).reshape(
            chunks, CHUNK, LANES
        )
    for i in range(2 * heads):
        piece = jnp.concatenate(
            [kv[:, i * hd : (i + 1) * hd], jnp.zeros((span, LANES - hd), bf16)], axis=1
        )
        cache[i * blocks : (i + 1) * blocks, 0:KV_CHUNK, :] = piece.reshape(blocks, KV_CHUNK, LANES)
    for i in range(2 * heads):
        rest = slice(i * LANES + hd, (i + 1) * LANES)
        w_own[rest, :] = jnp.zeros((LANES - hd, half), bf16)
        w_other[rest, :] = jnp.zeros((LANES - hd, half), bf16)

    loads[1].wait()
    feats = jnp.dot(normed[...], w_feature[...], preferred_element_type=f32)
    both_t = jnp.concatenate(halves(jnp.transpose(feats)), axis=0)
    both = jnp.concatenate(halves(feats), axis=1)
    channels = feats.shape[1]
    feat[...] = both[:, 0:channels]
    feat_t[...] = both_t[0:channels, :]
    loads[2].wait()
    for copy in own_w:
        copy.start()
    for lo in range(0, w_value.shape[1], 256):
        up = min(lo + 256, w_value.shape[1])
        wide[:, lo:up] = jnp.dot(
            normed[...], w_value[:, lo:up], preferred_element_type=f32
        ).astype(bf16)
    lane = lax.broadcasted_iota(jnp.int32, (rows, LANES - hd), 1)
    ones = jnp.where(lane == 0, 1.0, 0.0).astype(bf16)
    zeros = jnp.zeros((rows, LANES - hd), bf16)
    for h in range(heads):
        at = 2 * h * hd
        lin_vals[h] = jnp.concatenate([wide[:, at : at + hd], ones], axis=1)
    pl.semaphore_wait(barrier, count - 1 + grp_count - 1 + 1)
    each_near(lambda peer: near_copy(peer, my_near).start())
    got_near[my_near] = cache[pl.ds(my_near * far, far)]

    token = lax.broadcasted_iota(jnp.int32, (1, rows), 1)
    keep = jnp.where(token >= start_of(anchor + rows - 1) - anchor, 1.0, 0.0)
    for h in range(heads):
        channel = (
            lax.broadcasted_iota(jnp.int32, (padded, 2 * channels), 1) % channels - h * 2 * fd
        ).astype(f32)
        one = jnp.where((channel == tab_col[:, 2:3]) & (channel >= 0.0), 1.0, 0.0).astype(bf16)
        two = jnp.where((channel == tab_col[:, 3:4]) & (channel >= 0.0), 1.0, 0.0).astype(bf16)
        left = jnp.dot(one, both_t, preferred_element_type=f32) + tab_col[:, 4:5]
        right = jnp.dot(two, both_t, preferred_element_type=f32) + tab_col[:, 5:6]
        phi_t = (left * right * tab_col[:, 6:7] * keep).astype(bf16)
        own = jnp.dot(phi_t, lin_vals[h], preferred_element_type=f32)
        parts[h * chunks : (h + 1) * chunks] = pack_new(own, hd).reshape(chunks, CHUNK, LANES)
    each_seq(lambda peer: part_copy(peer, me).start())
    got_parts[me] = parts[me]

    owner = owners[row]
    each_near(lambda peer: near_copy(peer, peer).wait_recv())
    quarter[...] = got_near[owner % NEAR]
    each_far(lambda peer: far_copy(peer, my_far).start())
    got_far[my_far] = quarter[my_far]
    for copy in sent_w:
        copy.start()

    for h in range(heads):
        at = 2 * h * hd
        win_kv[2 * h + 1] = jnp.concatenate([wide[:, at + hd : at + 2 * hd], zeros], axis=1)
    last_load.wait()
    for lo in range(0, w_window.shape[1], 256):
        up = min(lo + 256, w_window.shape[1])
        wide[:, lo:up] = jnp.dot(
            normed[...], w_window[:, lo:up], preferred_element_type=f32
        ).astype(bf16)
    for h in range(heads):
        at = 2 * h * hd
        win_q[h] = jnp.concatenate([wide[:, at : at + hd], zeros], axis=1)
        win_kv[2 * h] = jnp.concatenate([wide[:, at + hd : at + 2 * hd], zeros], axis=1)
    rim_copy.start()

    each_far(lambda peer: far_copy(peer, peer).wait_recv())
    mine[...] = got_far[owner // NEAR]
    each_row(lambda peer: row_copy(peer, row).start())
    got_rows[row] = mine[...]

    for h in range(heads):
        channel = (
            lax.broadcasted_iota(jnp.int32, (2 * channels, padded), 0) % channels - h * 2 * fd
        ).astype(f32)
        one = jnp.where((channel == tab_row[0:1, :]) & (channel >= 0.0), 1.0, 0.0).astype(bf16)
        two = jnp.where((channel == tab_row[1:2, :]) & (channel >= 0.0), 1.0, 0.0).astype(bf16)
        left = jnp.dot(both, one, preferred_element_type=f32) + tab_row[4:5, :]
        right = jnp.dot(both, two, preferred_element_type=f32) + tab_row[5:6, :]
        phi_q[:, h * padded : (h + 1) * padded] = (left * right * tab_row[6:7, :]).astype(bf16)

    each_row(lambda peer: row_copy(peer, peer).wait_recv())
    base[my_near * far + my_far] = got_rows[groups[row]]
    each_far(lambda peer: base_far_copy(peer, my_far).start())

    tile = 128
    begins = []
    for b in range(rows // tile):
        place = lax.broadcasted_iota(jnp.int32, (tile, 1), 0) + (b * tile + anchor)
        best = jnp.zeros((tile, 1), jnp.int32)
        for start in starts:
            best = jnp.maximum(best, jnp.where(start <= place, start, 0))
        begins.append(best - anchor)

    def within(b):
        first, seen = b * tile, (b + 1) * tile
        tokens = lax.broadcasted_iota(jnp.int32, (tile, 1), 0) + first
        key_at = lax.broadcasted_iota(jnp.int32, (tile, seen), 1)
        causal = (key_at <= tokens) & (key_at >= begins[b])
        for h in range(heads):
            q = feat[first:seen, h * 2 * fd : h * 2 * fd + fd]
            k_t = feat_t[h * 2 * fd + fd : (h + 1) * 2 * fd, 0:seen]
            similar = jnp.dot(q, k_t, preferred_element_type=f32) * (1.0 / math.sqrt(fd))
            mass = jnp.where(causal, 1.0 + similar + 0.5 * similar * similar, 0.0)
            intra[h, first:seen, :] = jnp.dot(
                mass.astype(bf16), lin_vals[h, 0:seen, :], preferred_element_type=f32
            )

    within(3)

    each_seq(lambda peer: part_copy(peer, peer).wait_recv())

    def scan(i, carry):
        for j in range(8):
            k = i * 8 + j
            results[k] = pack_sum(carry, hd)
            carry = carry * restarts[k] + got_parts[k].astype(f32)
        return carry

    lax.fori_loop(0, count // 8, scan, jnp.zeros((CHUNK, LANES), f32))
    each_seq(lambda peer: result_copy(peer, me).start())
    carried[me] = results[me]

    each_far(lambda peer: base_far_copy(peer, peer).wait_recv())
    for kind in range(2):
        for copy in slabs[kind, 0]:
            copy.start()
    within(0)
    within(1)
    for kind in range(2):
        slab_arrived(kind, 0)
        for copy in slabs[kind, 1]:
            copy.start()
    within(2)

    slab_arrived(0, 1)
    rim_copy.wait()
    for h in range(heads):
        for b in range(rows // tile):
            first = b * tile
            tokens = lax.broadcasted_iota(jnp.int32, (tile, 1), 0) + first
            slot = lax.broadcasted_iota(jnp.int32, (tile, 2 * span + tile), 1)
            near_at = slot + (first - 2 * span)
            early = (slot < span) & (slot >= tokens - begins[b] + 1)
            band = (
                (slot >= span) & (near_at <= tokens) & (near_at > tokens - span)
                & (near_at >= begins[b])
            )
            sides = []
            for i in (2 * h, 2 * h + 1):
                cached = base[i * blocks : (i + 1) * blocks, 0:KV_CHUNK, :].reshape(span, LANES)
                if b == 0:
                    recent = [rim[i], win_kv[i, 0:tile, :]]
                else:
                    recent = [win_kv[i, first - span : first + tile, :]]
                sides.append(jnp.concatenate([cached] + recent, axis=0))
            scores = lax.dot_general(
                win_q[h, first : first + tile, :], sides[0], contract, preferred_element_type=f32
            ) * (1.0 / math.sqrt(hd))
            scores = jnp.where(early | band, scores, -1e30)
            weights = jnp.exp(scores - jnp.max(scores, axis=1, keepdims=True))
            weights = (weights / jnp.sum(weights, axis=1, keepdims=True)).astype(bf16)
            win_out = jnp.dot(weights, sides[1], preferred_element_type=f32)
            attended[first : first + tile, (2 * h + 1) * LANES : (2 * h + 2) * LANES] = (
                win_out.astype(bf16)
            )
        across[2 * h + 1].start()

    slab_arrived(1, 1)
    each_seq(lambda peer: result_copy(peer, peer).wait_recv())
    for h in range(heads):
        own = slice(h * chunks, (h + 1) * chunks)
        from_base = base[own, KV_CHUNK:, :].reshape(padded, LANES)
        from_carry = carried[own].reshape(padded, LANES)
        for b in range(rows // tile):
            at = slice(b * tile, (b + 1) * tile)
            use_carry = jnp.where(begins[b] < 0, 1.0, 0.0)
            phi = phi_q[at, h * padded : (h + 1) * padded]
            mixed = intra[h, at, :] + jnp.dot(phi, from_base, preferred_element_type=f32)
            mixed = mixed + use_carry * jnp.dot(phi, from_carry, preferred_element_type=f32)
            below = mixed[:, hd : hd + 1] + mixed[:, hd + 1 : hd + 2]
            lane = lax.broadcasted_iota(jnp.int32, (tile, LANES), 1)
            attended[at, 2 * h * LANES : (2 * h + 1) * LANES] = jnp.where(
                lane < hd, mixed / below, 0.0
            ).astype(bf16)
        across[2 * h].start()

    for copy in own_w:
        copy.wait()
    for lo in range(0, half, 256):
        up = min(lo + 256, half)
        residual = hidden[:, pl.ds(pl.multiple_of(core * half + lo, LANES), up - lo)].astype(f32)
        out[:, lo:up] = residual + jnp.dot(
            attended[...], w_own[:, lo:up], preferred_element_type=f32
        )
    for copy in sent_w:
        copy.wait()
    for copy in across:
        copy.wait()
    for lo in range(0, half, 256):
        up = min(lo + 256, half)
        out[:, lo:up] += jnp.dot(from_other[...], w_other[:, lo:up], preferred_element_type=f32)
    each_near(lambda peer: near_copy(peer, my_near).wait_send())
    each_far(lambda peer: far_copy(peer, my_far).wait_send())
    each_row(lambda peer: row_copy(peer, row).wait_send())
    each_far(lambda peer: base_far_copy(peer, my_far).wait_send())
    for copies in slabs.values():
        for copy in copies:
            copy.wait_send()
    each_seq(lambda peer: part_copy(peer, me).wait_send())
    each_seq(lambda peer: result_copy(peer, me).wait_send())


def local(
    hidden_in, norm_gain, w_feature, w_value, w_window, w_out,
    prefix_state, prefix_norm, prefix_kv, lengths, prefix_owner, row_group,
):
    heads, nf, hd = prefix_state.shape[2:]
    fd = w_feature.shape[1] // (2 * heads)
    rows, width = hidden_in.shape[1:]
    span = prefix_kv.shape[2]
    count, groups = lax.axis_size("seq"), lax.axis_size("grp")
    far = count // NEAR
    chunks = count // heads
    columns = width // lax.axis_size("tp")
    tab = feature_tables(fd, chunks)
    both = CHUNK + KV_CHUNK
    dma = pltpu.SemaphoreType.DMA

    def pair(n):
        return [dma((n,)), dma((n,))]

    def vm(*dims, dtype=bf16):
        return pltpu.VMEM(dims, dtype)

    vmem = pl.BlockSpec(memory_space=pltpu.VMEM)
    smem = pl.BlockSpec(memory_space=pltpu.SMEM)
    anywhere = pl.BlockSpec(memory_space=pl.ANY)
    mixed = pl.pallas_call(
        functools.partial(kernel, (heads, nf, hd, fd, count)),
        out_shape=jax.ShapeDtypeStruct((rows, columns), f32),
        in_specs=[smem] * 3
        + [anywhere, vmem] + [anywhere] * 5 + [vmem, anywhere, vmem, vmem],
        out_specs=vmem,
        scratch_shapes=[
            pltpu.SMEM((count,), f32), vm(heads, nf, hd, dtype=f32), vm(span, 2 * heads * hd),
            vm(rows, width), vm(width, 2 * heads * fd),
            vm(width, 2 * heads * hd), vm(width, 2 * heads * hd),
            vm(rows, width), vm(rows, 2 * heads * hd),
            vm(rows, heads * chunks * CHUNK), vm(rows, 2 * heads * fd), vm(2 * heads * fd, rows),
            vm(heads, rows, LANES), vm(heads, rows, LANES), vm(2 * heads, rows, LANES),
            vm(heads, rows, LANES, dtype=f32),
            vm(count, both, LANES), vm(count, CHUNK, LANES),
            vm(NEAR, far, both, LANES), vm(far, both, LANES), vm(far, both, LANES),
            vm(both, LANES), vm(groups, both, LANES), vm(count, both, LANES),
            vm(count, CHUNK, LANES), vm(count, CHUNK, LANES), vm(count, CHUNK, LANES),
            vm(2 * heads, span, LANES),
            vm(rows, 2 * heads * LANES), vm(rows, 2 * heads * LANES),
            vm(2 * heads * LANES, columns), vm(2 * heads * LANES, columns),
            dma((5 + heads,)), dma((2 * heads,)),
        ]
        + pair(2 * heads) + pair(2 * heads)
        + pair(NEAR) + pair(far) + pair(groups) + pair(far) + pair(8)
        + pair(count) + pair(count) + [dma((2,))],
        compiler_params=pltpu.CompilerParams(
            collective_id=0, has_side_effects=True, vmem_limit_bytes=60 * 1024 * 1024
        ),
        name="mixers",
    )(
        lengths, prefix_owner, row_group,
        hidden_in[0], norm_gain, w_feature, w_value, w_window, w_out,
        jnp.swapaxes(prefix_state[0, 0], 0, 1), prefix_norm[0, 0], prefix_kv[0, 0],
        jnp.asarray(tab), jnp.asarray(np.ascontiguousarray(tab.T)),
    )
    return mixed[None]


def solution(mesh):
    placed = (
        P("grp", "seq", None),
        P(),
        P(None, "tp"),
        P(None, "tp"),
        P(None, "tp"),
        P("tp", None),
        P("grp", "seq", "tp", None, None),
        P("grp", "seq", "tp", None),
        P("grp", "seq", None, "tp"),
        P("grp", None),
        P(),
        P(),
    )
    return jax.shard_map(
        local, mesh=mesh, in_specs=placed, out_specs=P("grp", "seq", "tp"), check_vma=False
    )
```
